32 devices in a mesh: cuts: 2 (over x), tile: 16 (over z, y, core).
Axes of the slice: x: 2, y: 2, z: 4, core: 2. Of those that a mesh axis runs over, the one named last changes fastest.
Arguments:
- object_delta: float32 [2, 2, 2048, 4096], P('cuts', None, None, 'tile'), may hold values from -1.2 to 1.2
- probe_wave: bfloat16 [2, 256, 256], replicated, may hold values from -4 to 4
- intensity: float32 [32, 256, 256], P('tile'), may hold values from 0 to 2
- positions: int32 [32, 2], P('tile'), may hold values from 0 to 3840, as said below
Outputs:
- object_gradient: float32 [2, 2, 2048, 4096], P('cuts', None, None, 'tile')
The draws below stay inside these ranges and needn't reach their ends.
Inputs may be any that keep to these rules, and one draw needn't show every extreme that they name: `positions`: row entries run from 0 to 1792. The column of probe k lies in columns (k // 2) * 256 to (k // 2) * 256 + 255, and equals (k // 2) * 256 for the probes of the last block of 2.
All inputs are finite; a program needn't handle non-finite values.
Results may differ from the reference program's by a relative error of at most 0.04.
Values may be sent and summed in bfloat16 or wider, within the bound.
A program may use at most 64 MiB of HBM per device.

```python
import math
import jax
import jax.numpy as jnp
from jax import lax

PROBE = 256
PR_DEV = 2
OBJ_ROWS = 2048
TILE_COLS = 256
SLICES = 2
PROBES = 32
OBJ_COLS = 4096


def draw_positions(key, part):
    row_key = jax.random.fold_in(key, 101)
    column_key = jax.random.fold_in(key, 202)
    corner_rows = jax.random.randint(row_key, (PROBES,), 0, OBJ_ROWS - PROBE + 1, dtype=jnp.int32)
    corner_rows = corner_rows.at[0].set(0).at[PROBES - 1].set(OBJ_ROWS - PROBE)
    owner_tile = jnp.arange(PROBES, dtype=jnp.int32) // PR_DEV
    offset = jax.random.randint(column_key, (PROBES,), 0, TILE_COLS, dtype=jnp.int32)
    offset = jnp.where(owner_tile == PROBES // PR_DEV - 1, 0, offset)
    corner_cols = owner_tile * TILE_COLS + offset
    return jnp.stack([corner_rows, corner_cols], axis=1).astype(jnp.int32)


def block_scale(rng, extent, shards, low, largest):
    level, own = 1.0, jax.random.fold_in(rng, 6)
    for dim, shards_of in shards:
        steps = jnp.exp(jax.random.uniform(jax.random.fold_in(own, dim), (shards_of,), jnp.float32, low / len(shards), largest / len(shards)))
        level = level * jnp.repeat(steps, extent[dim] // shards_of).reshape([-1 if axis == dim else 1 for axis in range(len(extent))])
    return level


def centred(rng, dims, spread, reach, pieces=(), kind=jnp.bfloat16):
    gain = block_scale(rng, dims, pieces, -0.22, 0.18) if pieces else 1.0
    entries = jax.random.normal(rng, dims, jnp.float32) * spread * gain
    return jnp.minimum(jnp.maximum(entries, -reach), reach).astype(kind)


def setup_inputs(seed: int = 0) -> dict:
    streams_of = jax.random.split(jax.random.key(seed), 5)
    object_delta = centred(streams_of[0], (SLICES, 2, OBJ_ROWS, OBJ_COLS), 0.2, 1.2, ((0, 2), (3, 16)), jnp.float32)
    probe_wave = centred(streams_of[1], (2, PROBE, PROBE), 0.6, 4.0)
    intensity = jnp.clip(2.0 * jax.random.uniform(streams_of[2], (PROBES, PROBE, PROBE), jnp.float32) ** block_scale(streams_of[2], (PROBES, PROBE, PROBE), ((0, 16),), -0.2, 0.2), 0.0, 2.0)
    positions = draw_positions(jax.random.fold_in(streams_of[4], 71), 0)
    return {"object_delta": object_delta, "probe_wave": probe_wave, "intensity": intensity, "positions": positions}


HIGHEST = lax.Precision.HIGHEST

def make_tables(probe_width):
    counter = jnp.arange(probe_width, dtype=jnp.int32)
    phase_table = (counter[:, None] * counter[None, :] % probe_width).astype(jnp.float32) * (2.0 * math.pi / probe_width)
    norm_scale = 1.0 / math.sqrt(probe_width)
    four_re = jnp.cos(phase_table) * norm_scale
    four_im = -jnp.sin(phase_table) * norm_scale
    signed = jnp.where(counter < probe_width // 2, counter, counter - probe_width).astype(jnp.float32)
    kernel_phase = -2.0 * math.pi / probe_width * signed * signed
    kernel_re = jnp.cos(kernel_phase)[:, None]
    kernel_im = jnp.sin(kernel_phase)[:, None]
    scaled_re = kernel_re * four_re - kernel_im * four_im
    scaled_im = kernel_re * four_im + kernel_im * four_re
    prop_re = (jnp.dot(four_re, scaled_re, precision=HIGHEST) + jnp.dot(four_im, scaled_im, precision=HIGHEST)).astype(jnp.bfloat16)
    prop_im = (jnp.dot(four_re, scaled_im, precision=HIGHEST) - jnp.dot(four_im, scaled_re, precision=HIGHEST)).astype(jnp.bfloat16)
    four_re = four_re.astype(jnp.bfloat16)
    four_im = four_im.astype(jnp.bfloat16)
    far_forward = ((four_re, four_im), (four_re, four_im))
    far_adjoint = ((four_re, -four_im), (four_re, -four_im))
    prop_forward = ((prop_re, prop_im), (prop_re.T, prop_im.T))
    prop_adjoint = ((prop_re.T, -prop_im.T), (prop_re, -prop_im))
    return (far_forward, far_adjoint, prop_forward, prop_adjoint)

def complex_dot(left_re, left_im, right_re, right_im):
    real_part = jnp.dot(left_re, right_re, preferred_element_type=jnp.float32) - jnp.dot(left_im, right_im, preferred_element_type=jnp.float32)
    imag_part = jnp.dot(left_re, right_im, preferred_element_type=jnp.float32) + jnp.dot(left_im, right_re, preferred_element_type=jnp.float32)
    return (real_part, imag_part)

def sandwich(wave_re, wave_im, operands):
    (left_re, left_im), (right_re, right_im) = operands
    inner_re, inner_im = complex_dot(left_re, left_im, wave_re, wave_im)
    return complex_dot(inner_re.astype(jnp.bfloat16), inner_im.astype(jnp.bfloat16), right_re, right_im)

def probe_gradient(object_delta, probe_wave, intensity_one, corner_row, corner_col, tables):
    far_forward, far_adjoint, prop_forward, prop_adjoint = tables
    anchor = jnp.zeros((), jnp.int32)
    patches = lax.dynamic_slice(object_delta, (anchor, anchor, corner_row, corner_col), (object_delta.shape[0], 2, PROBE, PROBE))

    def forward_step(wave_in, patch_now):
        trans_re = 1.0 + patch_now[0]
        trans_im = patch_now[1]
        wave_re = wave_in[0].astype(jnp.float32)
        wave_im = wave_in[1].astype(jnp.float32)
        exit_re = wave_re * trans_re - wave_im * trans_im
        exit_im = wave_re * trans_im + wave_im * trans_re
        out_re, out_im = sandwich(exit_re.astype(jnp.bfloat16), exit_im.astype(jnp.bfloat16), prop_forward)
        return (jnp.stack([out_re, out_im]).astype(jnp.bfloat16), wave_in)
    final_wave, stored = lax.scan(forward_step, probe_wave, patches)
    far_re, far_im = sandwich(final_wave[0], final_wave[1], far_forward)
    misfit = far_re * far_re + far_im * far_im - intensity_one
    seed_re, seed_im = sandwich((misfit * far_re).astype(jnp.bfloat16), (misfit * far_im).astype(jnp.bfloat16), far_adjoint)
    seed_wave = jnp.stack([seed_re, seed_im]).astype(jnp.bfloat16)

    def adjoint_step(adjoint_in, scan_pair):
        stored_now, patch_now = scan_pair
        back_re, back_im = sandwich(adjoint_in[0], adjoint_in[1], prop_adjoint)
        wave_re = stored_now[0].astype(jnp.float32)
        wave_im = stored_now[1].astype(jnp.float32)
        grad_re = wave_re * back_re + wave_im * back_im
        grad_im = wave_re * back_im - wave_im * back_re
        trans_re = 1.0 + patch_now[0]
        trans_im = patch_now[1]
        new_re = trans_re * back_re + trans_im * back_im
        new_im = trans_re * back_im - trans_im * back_re
        return (jnp.stack([new_re, new_im]).astype(jnp.bfloat16), jnp.stack([grad_re, grad_im]))
    _, gradients = lax.scan(adjoint_step, seed_wave, (stored, patches), reverse=True)
    return gradients

def reference(object_delta, probe_wave, intensity, positions):
    tables = make_tables(PROBE)
    initial = jnp.zeros(object_delta.shape, jnp.float32)

    def accumulate(running, scan_item):
        intensity_one, corner = scan_item
        corner_row = corner[0]
        corner_col = corner[1]
        gradients = probe_gradient(object_delta, probe_wave, intensity_one, corner_row, corner_col, tables)
        anchor = jnp.zeros((), jnp.int32)
        start_at = (anchor, anchor, corner_row, corner_col)
        previous = lax.dynamic_slice(running, start_at, gradients.shape)
        return (lax.dynamic_update_slice(running, previous + gradients, start_at), None)
    result, _ = lax.scan(accumulate, initial, (intensity, positions))
    return result
```

```python
import functools
import math

import jax
import jax.numpy as jnp
import numpy as np
from jax import lax
from jax.experimental import pallas as pl
from jax.experimental.pallas import tpu as pltpu
from jax.sharding import PartitionSpec as P

F32 = jnp.float32
BF16 = jnp.bfloat16
MESH = pl.DeviceIdType.MESH
LANE_ROWS = 8


def make_tables(width):
    counter = np.arange(width)
    phase = (counter[:, None] * counter[None, :] % width) * (2.0 * math.pi / width)
    four = np.exp(-1j * phase) / math.sqrt(width)
    signed = np.where(counter < width // 2, counter, counter - width).astype(np.float64)
    kernel = np.exp(-2j * math.pi / width * signed * signed)
    prop = np.conj(four) @ (kernel[:, None] * four)
    prop = 0.5 * (prop + prop.T)

    def block(table):
        re, im = table.real, table.imag
        return np.block([[re, -im], [im, re]])

    big = [block(prop), block(prop).T, block(four), block(four).T]
    return np.stack(big).astype(np.float32).astype(jnp.bfloat16)


def dot(a, b):
    return jnp.dot(a, b, preferred_element_type=F32)


def repeat(count, body):
    if count == 1:
        body(0)
    elif count > 1:
        lax.fori_loop(0, count, lambda i, _: (body(i), 0)[1], 0)


def exchange_kernel(
    obj_hbm, probe_hbm, inten_hbm, pos, tabs_hbm,
    own_out, strip_out, left_out,
    obj_v, obj_b, probe_v, inten_v, tabs_v, strip_send, strip_recv, win, psi, lam, grad_send,
    load_sem, pos_sem, strip_ssem, strip_rsem, x_ssem, x_rsem, g_ssem, g_rsem,
    *, chunks, gchunks,
):
    cut, tile = lax.axis_index("cuts"), lax.axis_index("tile")
    ncut, ntile = lax.axis_size("cuts"), lax.axis_size("tile")
    per, _, rows, cols = obj_v.shape
    count, width = inten_v.shape[0], inten_v.shape[1]
    total = ncut * per
    height = width // chunks
    gheight = width // gchunks
    has_left, has_right = tile > 0, tile < ntile - 1
    left, right = {"tile": tile - 1}, {"tile": tile + 1}

    obj_copy = pltpu.make_async_copy(obj_hbm, obj_v, load_sem.at[0])
    probe_copy = pltpu.make_async_copy(probe_hbm, probe_v, load_sem.at[1])
    tabs_copy = pltpu.make_async_copy(tabs_hbm, tabs_v, load_sem.at[2])
    inten_copy = pltpu.make_async_copy(inten_hbm, inten_v, load_sem.at[3])
    obj_copy.start()
    probe_copy.start()
    tabs_copy.start()
    inten_copy.start()

    barrier = pltpu.get_barrier_semaphore()

    @pl.when(has_left)
    def _():
        pl.semaphore_signal(barrier, inc=1, device_id=left, device_id_type=MESH)

    @pl.when(has_right)
    def _():
        pl.semaphore_signal(barrier, inc=1, device_id=right, device_id_type=MESH)

    for o in range(1, ncut):
        peer = {"cuts": lax.rem(cut + o, ncut)}
        pl.semaphore_signal(barrier, inc=1, device_id=peer, device_id_type=MESH)
    peers = ncut - 1 + jnp.where(has_left, 1, 0) + jnp.where(has_right, 1, 0)
    pl.semaphore_wait(barrier, peers)

    pos_copy = pltpu.make_async_remote_copy(
        src_ref=pos, dst_ref=left_out, send_sem=pos_sem.at[0], recv_sem=pos_sem.at[1],
        device_id=right, device_id_type=MESH,
    )

    @pl.when(has_right)
    def _():
        pos_copy.start()

    lanes = lax.broadcasted_iota(jnp.int32, (height, cols), 1)
    glanes = lax.broadcasted_iota(jnp.int32, (gheight, cols), 1)
    cell = lax.broadcasted_iota(jnp.int32, (width, rows), 1)
    line = lax.broadcasted_iota(jnp.int32, (width, rows), 0)

    def window_rows(row):
        base = row // LANE_ROWS * LANE_ROWS
        wanted = base + line + jnp.where(line < row - base, width, 0)
        pick = jnp.where(cell == wanted, 1.0, 0.0).astype(BF16)
        return dot(pick, obj_b[...]).astype(BF16)

    def strip_copy(p, k):
        span = pl.ds(k * height, height)
        return pltpu.make_async_remote_copy(
            src_ref=strip_send.at[p, :, :, span, :], dst_ref=strip_recv.at[p, :, :, span, :],
            send_sem=strip_ssem.at[p, k], recv_sem=strip_rsem.at[p, k],
            device_id=left, device_id_type=MESH,
        )

    def cross_copy(o, source, p, k):
        span = pl.ds(k * height, height)
        part = win.at[p, source, :, :, span, :]
        return pltpu.make_async_remote_copy(
            src_ref=part, dst_ref=part,
            send_sem=x_ssem.at[o - 1, p, k], recv_sem=x_rsem.at[o - 1, p, k],
            device_id={"cuts": lax.rem(cut + o, ncut)}, device_id_type=MESH,
        )

    def grad_copy(p, k):
        span = pl.ds(k * gheight, gheight)
        return pltpu.make_async_remote_copy(
            src_ref=grad_send.at[p, :, :, span, :], dst_ref=strip_out.at[p, :, :, span, :],
            send_sem=g_ssem.at[p, k], recv_sem=g_rsem.at[p, k],
            device_id=right, device_id_type=MESH,
        )

    probe_copy.wait()
    across = lax.broadcasted_iota(jnp.int32, (width, width), 1)
    down = lax.broadcasted_iota(jnp.int32, (width, width), 0)
    for p in range(count):
        row, col = pos[p, 0], pos[p, 1] - tile * cols
        shift = row - row // LANE_ROWS * LANE_ROWS
        source = across + shift
        move_rows = jnp.where(jnp.where(source >= width, source - width, source) == down, 1.0, 0.0)
        source = down + col
        move_cols = jnp.where(jnp.where(source >= width, source - width, source) == across, 1.0, 0.0)
        for part in range(2):
            moved = dot(move_rows.astype(BF16), probe_v[part]).astype(BF16)
            psi[p, 0, part] = dot(moved, move_cols.astype(BF16)).astype(BF16)

    obj_copy.wait()
    for j in range(per):
        for part in range(2):
            side = pl.ds((2 * j + part) * cols, cols)
            obj_b[:, side] = obj_v[j, part].astype(BF16)

    @pl.when(has_left)
    def _():
        pos_copy.wait_recv()
        for p in range(count):
            picked = window_rows(left_out[p, 0])
            for j in range(per):
                for part in range(2):
                    first = (2 * j + part) * cols
                    strip_send[p, j, part] = picked[:, first : first + cols]
            for k in range(chunks):
                strip_copy(p, k).start()

    @pl.when(jnp.logical_not(has_left))
    def _():
        for p in range(count):
            for d in range(2):
                left_out[p, d] = 0
        strip_out[...] = jnp.zeros_like(strip_out)

    @pl.when(jnp.logical_not(has_right))
    def _():
        strip_recv[...] = jnp.zeros_like(strip_recv)

    for p in range(count):
        picked = window_rows(pos[p, 0])
        for j in range(per):
            for part in range(2):
                first = (2 * j + part) * cols
                win[p, cut, j, part] = picked[:, first : first + cols]

    for p in range(count):
        col = pos[p, 1] - tile * cols
        for k in range(chunks):

            @pl.when(has_right)
            def _():
                strip_copy(p, k).wait_recv()

            span = pl.ds(k * height, height)
            for j in range(per):
                for part in range(2):
                    win[p, cut, j, part, span, :] = jnp.where(
                        lanes >= col,
                        win[p, cut, j, part, span, :].astype(F32),
                        strip_recv[p, j, part, span, :].astype(F32),
                    ).astype(BF16)
            for o in range(1, ncut):
                cross_copy(o, cut, p, k).start()

    tabs_copy.wait()
    inten_copy.wait()

    def arrive(p, owner):
        @pl.when(owner != cut)
        def _():
            o = lax.rem(cut - owner + ncut, ncut)
            for k in range(chunks):
                cross_copy(o, owner, p, k).wait_recv()

    def sandwich(first, second, stacked):
        inner = dot(tabs_v[first], stacked).astype(BF16)
        side = jnp.concatenate([inner[:width], inner[width:]], axis=1)
        return dot(side, tabs_v[second])

    def exit_wave(p, s):
        owner, j = s // per, lax.rem(s, per)
        t_re = 1.0 + win[p, owner, j, 0].astype(F32)
        t_im = win[p, owner, j, 1].astype(F32)
        p_re, p_im = psi[p, s, 0].astype(F32), psi[p, s, 1].astype(F32)
        x_re = (p_re * t_re - p_im * t_im).astype(BF16)
        x_im = (p_re * t_im + p_im * t_re).astype(BF16)
        return jnp.concatenate([x_re, x_im], axis=0)

    def adjoint_slice(p, s, first, second, stacked):
        owner, j = s // per, lax.rem(s, per)
        col = pos[p, 1] - tile * cols
        inner = dot(tabs_v[first], stacked).astype(BF16)
        side = jnp.concatenate([inner[:width], inner[width:]], axis=1)

        @pl.when(owner == cut)
        def _():
            for k in range(gchunks):
                span = pl.ds(k * gheight, gheight)
                mu = dot(side[k * gheight : (k + 1) * gheight], tabs_v[second])
                m_re, m_im = mu[:, :width], mu[:, width:]
                p_re = psi[p, s, 0, span, :].astype(F32)
                p_im = psi[p, s, 1, span, :].astype(F32)
                g = (p_re * m_re + p_im * m_im, p_re * m_im - p_im * m_re)
                for part in range(2):
                    own_out[p, j, part, span, :] = jnp.where(glanes >= col, g[part], 0.0)
                    grad_send[p, j, part, span, :] = jnp.where(glanes >= col, 0.0, g[part]).astype(
                        BF16
                    )
                if per == 1:

                    @pl.when(has_right)
                    def _():
                        grad_copy(p, k).start()

        @pl.when(s > cut * per)
        def _():
            mu = dot(side, tabs_v[second])
            m_re, m_im = mu[:, :width], mu[:, width:]
            t_re = 1.0 + win[p, owner, j, 0].astype(F32)
            t_im = win[p, owner, j, 1].astype(F32)
            lam[:width] = (t_re * m_re + t_im * m_im).astype(BF16)
            lam[width:] = (t_re * m_im - t_im * m_re).astype(BF16)

    def one_probe(p):
        def forward(s):
            arrive(p, s // per)
            out = sandwich(0, 1, exit_wave(p, s))
            psi[p, s + 1, 0] = out[:, :width].astype(BF16)
            psi[p, s + 1, 1] = out[:, width:].astype(BF16)

        def backward(i):
            s = total - 2 - i

            @pl.when(s >= cut * per)
            def _():
                adjoint_slice(p, s, 1, 0, lam[...])

        if per == 1:
            repeat(total - 1, forward)
            arrive(p, total - 1)
        else:
            for s in range(ncut):
                arrive(p, s)
        adjoint_slice(p, total - 1, 3, 2, far_field(p))
        repeat(total - 1, backward)
        if per > 1:
            for k in range(gchunks):

                @pl.when(has_right)
                def _():
                    grad_copy(p, k).start()

    def far_field(p):
        out = sandwich(2, 3, exit_wave(p, total - 1))
        f_re, f_im = out[:, :width], out[:, width:]
        misfit = f_re * f_re + f_im * f_im - inten_v[p]
        return jnp.concatenate([(misfit * f_re).astype(BF16), (misfit * f_im).astype(BF16)], axis=0)

    for p in range(count):
        one_probe(p)

    @pl.when(has_right)
    def _():
        pos_copy.wait_send()
        for p in range(count):
            for k in range(gchunks):
                grad_copy(p, k).wait_send()

    for p in range(count):
        for k in range(chunks):
            for o in range(1, ncut):
                cross_copy(o, cut, p, k).wait_send()

    @pl.when(has_left)
    def _():
        for p in range(count):
            for k in range(chunks):
                strip_copy(p, k).wait_send()
        for p in range(count):
            for k in range(gchunks):
                grad_copy(p, k).wait_recv()


def place_kernel(own, strip, pos, left, out_hbm, out_v, sem):
    per, _, rows, cols = out_v.shape
    count, width = own.shape[0], own.shape[3]
    out_v[...] = jnp.zeros_like(out_v)
    iota = lax.broadcasted_iota(jnp.int32, (LANE_ROWS, cols), 0)

    def add(source, row, p):
        base = row // LANE_ROWS * LANE_ROWS
        shift = row - base
        body = pl.multiple_of(base + LANE_ROWS, LANE_ROWS)
        base = pl.multiple_of(base, LANE_ROWS)
        after = pl.multiple_of(jnp.minimum(base + width, rows - LANE_ROWS), LANE_ROWS)
        rest = width - LANE_ROWS
        for j in range(per):
            for part in range(2):
                whole = source[p, j, part].astype(F32)
                out_v[j, part, pl.ds(body, rest), :] += whole[LANE_ROWS:]
                head = whole[:LANE_ROWS]
                out_v[j, part, pl.ds(base, LANE_ROWS), :] += jnp.where(iota >= shift, head, 0.0)
                out_v[j, part, pl.ds(after, LANE_ROWS), :] += jnp.where(iota < shift, head, 0.0)

    for p in range(count):
        add(own, pos[p, 0], p)
        add(strip, left[p, 0], p)
    copy = pltpu.make_async_copy(out_v, out_hbm, sem)
    copy.start()
    copy.wait()


def per_device(tables, object_delta, probe_wave, intensity, positions):
    per, _, rows, cols = object_delta.shape
    count, width = intensity.shape[0], intensity.shape[1]
    ncut = lax.axis_size("cuts")
    chunks, gchunks = 4, 2
    anywhere = pl.BlockSpec(memory_space=pl.ANY)
    vmem = pl.BlockSpec(memory_space=pltpu.VMEM)
    smem = pl.BlockSpec(memory_space=pltpu.SMEM)
    dma = pltpu.SemaphoreType.DMA
    piece = (count, per, 2, width, cols)
    others = max(ncut - 1, 1)
    own, strip, left = pl.pallas_call(
        functools.partial(exchange_kernel, chunks=chunks, gchunks=gchunks),
        out_shape=(
            jax.ShapeDtypeStruct(piece, F32),
            jax.ShapeDtypeStruct(piece, BF16),
            jax.ShapeDtypeStruct(positions.shape, positions.dtype),
        ),
        in_specs=[anywhere, anywhere, anywhere, smem, anywhere],
        out_specs=(vmem, vmem, smem),
        scratch_shapes=[
            pltpu.VMEM(object_delta.shape, F32),
            pltpu.VMEM((rows, per * 2 * cols), BF16),
            pltpu.VMEM(probe_wave.shape, BF16),
            pltpu.VMEM(intensity.shape, F32),
            pltpu.VMEM(tables.shape, BF16),
            pltpu.VMEM(piece, BF16),
            pltpu.VMEM(piece, BF16),
            pltpu.VMEM((count, ncut, per, 2, width, cols), BF16),
            pltpu.VMEM((count, ncut * per, 2, width, cols), BF16),
            pltpu.VMEM((2 * width, cols), BF16),
            pltpu.VMEM(piece, BF16),
            dma((4,)),
            dma((2,)),
            dma((count, chunks)),
            dma((count, chunks)),
            dma((others, count, chunks)),
            dma((others, count, chunks)),
            dma((count, gchunks)),
            dma((count, gchunks)),
        ],
        compiler_params=pltpu.CompilerParams(collective_id=0, has_side_effects=True),
        name="exchange",
    )(object_delta, probe_wave, intensity, positions, tables)
    return pl.pallas_call(
        place_kernel,
        out_shape=jax.ShapeDtypeStruct(object_delta.shape, F32),
        in_specs=[vmem, vmem, smem, smem],
        out_specs=anywhere,
        scratch_shapes=[pltpu.VMEM(object_delta.shape, F32), dma],
        name="place",
    )(own, strip, positions, left)


def solution(mesh):
    def whole(object_delta, probe_wave, intensity, positions):
        tables = jnp.asarray(make_tables(probe_wave.shape[-1]))
        return jax.shard_map(
            per_device,
            mesh=mesh,
            in_specs=(
                P(),
                P("cuts", None, None, "tile"),
                P(),
                P("tile", None, None),
                P("tile", None),
            ),
            out_specs=P("cuts", None, None, "tile"),
            check_vma=False,
        )(tables, object_delta, probe_wave, intensity, positions)

    return whole
```

```python
import functools
import math

import jax
import jax.numpy as jnp
import numpy as np
from jax import lax
from jax.experimental import pallas as pl
from jax.experimental.pallas import tpu as pltpu
from jax.sharding import PartitionSpec as P

F32 = jnp.float32
BF16 = jnp.bfloat16
MESH = pl.DeviceIdType.MESH
LANE_ROWS = 8


def make_tables(width):
    counter = np.arange(width)
    phase = (counter[:, None] * counter[None, :] % width) * (2.0 * math.pi / width)
    four = np.exp(-1j * phase) / math.sqrt(width)
    signed = np.where(counter < width // 2, counter, counter - width).astype(np.float64)
    kernel = np.exp(-2j * math.pi / width * signed * signed)
    prop = np.conj(four) @ (kernel[:, None] * four)
    prop = 0.5 * (prop + prop.T)

    def block(table):
        re, im = table.real, table.imag
        return np.block([[re, -im], [im, re]])

    big = [block(prop), block(prop).T, block(four), block(four).T]
    return np.stack(big).astype(np.float32).astype(jnp.bfloat16)


def dot(a, b):
    return jnp.dot(a, b, preferred_element_type=F32)


def repeat(count, body):
    if count == 1:
        body(0)
    elif count > 1:
        lax.fori_loop(0, count, lambda i, _: (body(i), 0)[1], 0)


def exchange_kernel(
    obj_hbm, probe_hbm, inten_hbm, pos, tabs_hbm,
    own_out, strip_out, left_out,
    obj_v, obj_b, probe_v, inten_v, tabs_v, strip_send, strip_recv, win, psi, lam, grad_send,
    obj_sem, load_sem, pos_sem, strip_ssem, strip_rsem, x_ssem, x_rsem, g_ssem, g_rsem,
    *, chunks, gchunks,
):
    cut, tile = lax.axis_index("cuts"), lax.axis_index("tile")
    ncut, ntile = lax.axis_size("cuts"), lax.axis_size("tile")
    per, _, rows, cols = obj_v.shape
    count, width = inten_v.shape[0], inten_v.shape[1]
    total = ncut * per
    height = width // chunks
    gheight = width // gchunks
    has_left, has_right = tile > 0, tile < ntile - 1
    left, right = {"tile": tile - 1}, {"tile": tile + 1}

    def obj_copy(j, part):
        return pltpu.make_async_copy(obj_hbm.at[j, part], obj_v.at[j, part], obj_sem.at[j, part])

    probe_copy = pltpu.make_async_copy(probe_hbm, probe_v, load_sem.at[1])
    tabs_copy = pltpu.make_async_copy(tabs_hbm, tabs_v, load_sem.at[2])
    inten_copy = pltpu.make_async_copy(inten_hbm, inten_v, load_sem.at[3])
    for j in range(per):
        for part in range(2):
            obj_copy(j, part).start()
    probe_copy.start()

    barrier = pltpu.get_barrier_semaphore()

    @pl.when(has_left)
    def _():
        pl.semaphore_signal(barrier, inc=1, device_id=left, device_id_type=MESH)

    @pl.when(has_right)
    def _():
        pl.semaphore_signal(barrier, inc=1, device_id=right, device_id_type=MESH)

    for o in range(1, ncut):
        peer = {"cuts": lax.rem(cut + o, ncut)}
        pl.semaphore_signal(barrier, inc=1, device_id=peer, device_id_type=MESH)
    peers = ncut - 1 + jnp.where(has_left, 1, 0) + jnp.where(has_right, 1, 0)
    pl.semaphore_wait(barrier, peers)

    pos_copy = pltpu.make_async_remote_copy(
        src_ref=pos, dst_ref=left_out, send_sem=pos_sem.at[0], recv_sem=pos_sem.at[1],
        device_id=right, device_id_type=MESH,
    )

    @pl.when(has_right)
    def _():
        pos_copy.start()

    lanes = lax.broadcasted_iota(jnp.int32, (height, cols), 1)
    glanes = lax.broadcasted_iota(jnp.int32, (gheight, cols), 1)
    unit = 128
    cell = lax.broadcasted_iota(jnp.int32, (width, unit), 1)
    line = lax.broadcasted_iota(jnp.int32, (width, unit), 0)

    def window_rows(row):
        base = row // LANE_ROWS * LANE_ROWS
        wanted = base + line + jnp.where(line < row - base, width, 0) - cell
        picks = [jnp.where(wanted == i * unit, 1.0, 0.0).astype(BF16) for i in range(rows // unit)]
        return dot(jnp.concatenate(picks, axis=1), obj_b[...]).astype(BF16)

    def strip_copy(p, k):
        span = pl.ds(k * height, height)
        return pltpu.make_async_remote_copy(
            src_ref=strip_send.at[p, :, :, span, :], dst_ref=strip_recv.at[p, :, :, span, :],
            send_sem=strip_ssem.at[p, k], recv_sem=strip_rsem.at[p, k],
            device_id=left, device_id_type=MESH,
        )

    def cross_copy(o, source, p, k):
        span = pl.ds(k * height, height)
        part = win.at[p, source, :, :, span, :]
        return pltpu.make_async_remote_copy(
            src_ref=part, dst_ref=part,
            send_sem=x_ssem.at[o - 1, p, k], recv_sem=x_rsem.at[o - 1, p, k],
            device_id={"cuts": lax.rem(cut + o, ncut)}, device_id_type=MESH,
        )

    def grad_copy(p, k):
        span = pl.ds(k * gheight, gheight)
        return pltpu.make_async_remote_copy(
            src_ref=grad_send.at[p, :, :, span, :], dst_ref=strip_out.at[p, :, :, span, :],
            send_sem=g_ssem.at[p, k], recv_sem=g_rsem.at[p, k],
            device_id=right, device_id_type=MESH,
        )

    for j in range(per):
        for part in range(2):
            obj_copy(j, part).wait()
            side = pl.ds((2 * j + part) * cols, cols)
            obj_b[:, side] = obj_v[j, part].astype(BF16)

    tabs_copy.start()
    inten_copy.start()

    @pl.when(has_left)
    def _():
        pos_copy.wait_recv()
        for p in range(count):
            picked = window_rows(left_out[p, 0])
            for j in range(per):
                for part in range(2):
                    first = (2 * j + part) * cols
                    strip_send[p, j, part] = picked[:, first : first + cols]
            for k in range(chunks):
                strip_copy(p, k).start()

    @pl.when(jnp.logical_not(has_left))
    def _():
        for p in range(count):
            for d in range(2):
                left_out[p, d] = 0
        strip_out[...] = jnp.zeros_like(strip_out)

    @pl.when(jnp.logical_not(has_right))
    def _():
        strip_recv[...] = jnp.zeros_like(strip_recv)

    for p in range(count):
        picked = window_rows(pos[p, 0])
        for j in range(per):
            for part in range(2):
                first = (2 * j + part) * cols
                win[p, cut, j, part] = picked[:, first : first + cols]

    for p in range(count):
        col = pos[p, 1] - tile * cols
        for k in range(chunks):

            @pl.when(has_right)
            def _():
                strip_copy(p, k).wait_recv()

            span = pl.ds(k * height, height)
            for j in range(per):
                for part in range(2):
                    win[p, cut, j, part, span, :] = jnp.where(
                        lanes >= col,
                        win[p, cut, j, part, span, :].astype(F32),
                        strip_recv[p, j, part, span, :].astype(F32),
                    ).astype(BF16)
            for o in range(1, ncut):
                cross_copy(o, cut, p, k).start()

    probe_copy.wait()
    across = lax.broadcasted_iota(jnp.int32, (width, width), 1)
    down = lax.broadcasted_iota(jnp.int32, (width, width), 0)
    for p in range(count):
        row, col = pos[p, 0], pos[p, 1] - tile * cols
        shift = row - row // LANE_ROWS * LANE_ROWS
        source = across + shift
        move_rows = jnp.where(jnp.where(source >= width, source - width, source) == down, 1.0, 0.0)
        source = down + col
        move_cols = jnp.where(jnp.where(source >= width, source - width, source) == across, 1.0, 0.0)
        for part in range(2):
            moved = dot(move_rows.astype(BF16), probe_v[part]).astype(BF16)
            psi[p, 0, part] = dot(moved, move_cols.astype(BF16)).astype(BF16)

    tabs_copy.wait()
    inten_copy.wait()

    def arrive(p, owner):
        @pl.when(owner != cut)
        def _():
            o = lax.rem(cut - owner + ncut, ncut)
            for k in range(chunks):
                cross_copy(o, owner, p, k).wait_recv()

    def sandwich(first, second, stacked):
        inner = dot(tabs_v[first], stacked).astype(BF16)
        side = jnp.concatenate([inner[:width], inner[width:]], axis=1)
        return dot(side, tabs_v[second])

    def exit_wave(p, s):
        owner, j = s // per, lax.rem(s, per)
        t_re = 1.0 + win[p, owner, j, 0].astype(F32)
        t_im = win[p, owner, j, 1].astype(F32)
        p_re, p_im = psi[p, s, 0].astype(F32), psi[p, s, 1].astype(F32)
        x_re = (p_re * t_re - p_im * t_im).astype(BF16)
        x_im = (p_re * t_im + p_im * t_re).astype(BF16)
        return jnp.concatenate([x_re, x_im], axis=0)

    def adjoint_slice(p, s, first, second, stacked):
        owner, j = s // per, lax.rem(s, per)
        col = pos[p, 1] - tile * cols
        inner = dot(tabs_v[first], stacked).astype(BF16)
        side = jnp.concatenate([inner[:width], inner[width:]], axis=1)

        @pl.when(owner == cut)
        def _():
            for k in range(gchunks):
                span = pl.ds(k * gheight, gheight)
                mu = dot(side[k * gheight : (k + 1) * gheight], tabs_v[second])
                m_re, m_im = mu[:, :width], mu[:, width:]
                p_re = psi[p, s, 0, span, :].astype(F32)
                p_im = psi[p, s, 1, span, :].astype(F32)
                g = (p_re * m_re + p_im * m_im, p_re * m_im - p_im * m_re)
                for part in range(2):
                    own_out[p, j, part, span, :] = jnp.where(glanes >= col, g[part], 0.0)
                    grad_send[p, j, part, span, :] = jnp.where(glanes >= col, 0.0, g[part]).astype(
                        BF16
                    )
                if per == 1:

                    @pl.when(has_right)
                    def _():
                        grad_copy(p, k).start()

        @pl.when(s > cut * per)
        def _():
            mu = dot(side, tabs_v[second])
            m_re, m_im = mu[:, :width], mu[:, width:]
            t_re = 1.0 + win[p, owner, j, 0].astype(F32)
            t_im = win[p, owner, j, 1].astype(F32)
            lam[:width] = (t_re * m_re + t_im * m_im).astype(BF16)
            lam[width:] = (t_re * m_im - t_im * m_re).astype(BF16)

    def one_probe(p):
        def forward(s):
            arrive(p, s // per)
            out = sandwich(0, 1, exit_wave(p, s))
            psi[p, s + 1, 0] = out[:, :width].astype(BF16)
            psi[p, s + 1, 1] = out[:, width:].astype(BF16)

        def backward(i):
            s = total - 2 - i

            @pl.when(s >= cut * per)
            def _():
                adjoint_slice(p, s, 1, 0, lam[...])

        if per == 1:
            repeat(total - 1, forward)
            arrive(p, total - 1)
        else:
            for s in range(ncut):
                arrive(p, s)
        adjoint_slice(p, total - 1, 3, 2, far_field(p))
        repeat(total - 1, backward)
        if per > 1:
            for k in range(gchunks):

                @pl.when(has_right)
                def _():
                    grad_copy(p, k).start()

    def far_field(p):
        out = sandwich(2, 3, exit_wave(p, total - 1))
        f_re, f_im = out[:, :width], out[:, width:]
        misfit = f_re * f_re + f_im * f_im - inten_v[p]
        return jnp.concatenate([(misfit * f_re).astype(BF16), (misfit * f_im).astype(BF16)], axis=0)

    for p in range(count):
        one_probe(p)

    @pl.when(has_right)
    def _():
        pos_copy.wait_send()
        for p in range(count):
            for k in range(gchunks):
                grad_copy(p, k).wait_send()

    for p in range(count):
        for k in range(chunks):
            for o in range(1, ncut):
                cross_copy(o, cut, p, k).wait_send()

    @pl.when(has_left)
    def _():
        for p in range(count):
            for k in range(chunks):
                strip_copy(p, k).wait_send()
        for p in range(count):
            for k in range(gchunks):
                grad_copy(p, k).wait_recv()


def place_kernel(own, strip, pos, left, out_hbm, out_v, sem):
    per, _, rows, cols = out_v.shape
    count, width = own.shape[0], own.shape[3]
    iota = lax.broadcasted_iota(jnp.int32, (LANE_ROWS, cols), 0)
    rest = width - LANE_ROWS

    def add(source, row, p, j, part):
        base = row // LANE_ROWS * LANE_ROWS
        shift = row - base
        body = pl.multiple_of(base + LANE_ROWS, LANE_ROWS)
        base = pl.multiple_of(base, LANE_ROWS)
        after = pl.multiple_of(jnp.minimum(base + width, rows - LANE_ROWS), LANE_ROWS)
        whole = source[p, j, part].astype(F32)
        out_v[j, part, pl.ds(body, rest), :] += whole[LANE_ROWS:]
        head = whole[:LANE_ROWS]
        out_v[j, part, pl.ds(base, LANE_ROWS), :] += jnp.where(iota >= shift, head, 0.0)
        out_v[j, part, pl.ds(after, LANE_ROWS), :] += jnp.where(iota < shift, head, 0.0)

    copies = []
    for j in range(per):
        for part in range(2):
            out_v[j, part] = jnp.zeros((rows, cols), F32)
            for p in range(count):
                add(own, pos[p, 0], p, j, part)
                add(strip, left[p, 0], p, j, part)
            copy = pltpu.make_async_copy(out_v.at[j, part], out_hbm.at[j, part], sem.at[j, part])
            copy.start()
            copies.append(copy)
    for copy in copies:
        copy.wait()


def per_device(tables, object_delta, probe_wave, intensity, positions):
    per, _, rows, cols = object_delta.shape
    count, width = intensity.shape[0], intensity.shape[1]
    ncut = lax.axis_size("cuts")
    chunks, gchunks = 4, 2
    anywhere = pl.BlockSpec(memory_space=pl.ANY)
    vmem = pl.BlockSpec(memory_space=pltpu.VMEM)
    smem = pl.BlockSpec(memory_space=pltpu.SMEM)
    dma = pltpu.SemaphoreType.DMA
    piece = (count, per, 2, width, cols)
    others = max(ncut - 1, 1)
    own, strip, left = pl.pallas_call(
        functools.partial(exchange_kernel, chunks=chunks, gchunks=gchunks),
        out_shape=(
            pltpu.VMEM(piece, F32),
            pltpu.VMEM(piece, BF16),
            jax.ShapeDtypeStruct(positions.shape, positions.dtype),
        ),
        in_specs=[anywhere, anywhere, anywhere, smem, anywhere],
        out_specs=(vmem, vmem, smem),
        scratch_shapes=[
            pltpu.VMEM(object_delta.shape, F32),
            pltpu.VMEM((rows, per * 2 * cols), BF16),
            pltpu.VMEM(probe_wave.shape, BF16),
            pltpu.VMEM(intensity.shape, F32),
            pltpu.VMEM(tables.shape, BF16),
            pltpu.VMEM(piece, BF16),
            pltpu.VMEM(piece, BF16),
            pltpu.VMEM((count, ncut, per, 2, width, cols), BF16),
            pltpu.VMEM((count, ncut * per, 2, width, cols), BF16),
            pltpu.VMEM((2 * width, cols), BF16),
            pltpu.VMEM(piece, BF16),
            dma((per, 2)),
            dma((4,)),
            dma((2,)),
            dma((count, chunks)),
            dma((count, chunks)),
            dma((others, count, chunks)),
            dma((others, count, chunks)),
            dma((count, gchunks)),
            dma((count, gchunks)),
        ],
        compiler_params=pltpu.CompilerParams(collective_id=0, has_side_effects=True),
        name="exchange",
    )(object_delta, probe_wave, intensity, positions, tables)
    own = pltpu.with_memory_space_constraint(own, pltpu.VMEM)
    strip = pltpu.with_memory_space_constraint(strip, pltpu.VMEM)
    return pl.pallas_call(
        place_kernel,
        out_shape=jax.ShapeDtypeStruct(object_delta.shape, F32),
        in_specs=[vmem, vmem, smem, smem],
        out_specs=anywhere,
        scratch_shapes=[pltpu.VMEM(object_delta.shape, F32), dma((per, 2))],
        name="place",
    )(own, strip, positions, left)


def solution(mesh):
    def whole(object_delta, probe_wave, intensity, positions):
        tables = jnp.asarray(make_tables(probe_wave.shape[-1]))
        return jax.shard_map(
            per_device,
            mesh=mesh,
            in_specs=(
                P(),
                P("cuts", None, None, "tile"),
                P(),
                P("tile", None, None),
                P("tile", None),
            ),
            out_specs=P("cuts", None, None, "tile"),
            check_vma=False,
        )(tables, object_delta, probe_wave, intensity, positions)

    return whole
```

```python
import functools
import math

import jax
import jax.numpy as jnp
import numpy as np
from jax import lax
from jax.experimental import pallas as pl
from jax.experimental.pallas import tpu as pltpu
from jax.sharding import PartitionSpec as P

F32 = jnp.float32
BF16 = jnp.bfloat16
MESH = pl.DeviceIdType.MESH
LANE_ROWS = 8


def make_tables(width):
    counter = np.arange(width)
    phase = (counter[:, None] * counter[None, :] % width) * (2.0 * math.pi / width)
    four = np.exp(-1j * phase) / math.sqrt(width)
    signed = np.where(counter < width // 2, counter, counter - width).astype(np.float64)
    kernel = np.exp(-2j * math.pi / width * signed * signed)
    prop = np.conj(four) @ (kernel[:, None] * four)
    prop = 0.5 * (prop + prop.T)

    def block(table):
        re, im = table.real, table.imag
        return np.block([[re, -im], [im, re]])

    big = [block(prop), block(prop).T, block(four), block(four).T]
    return np.stack(big).astype(np.float32).astype(jnp.bfloat16)


def dot(a, b):
    return jnp.dot(a, b, preferred_element_type=F32)


def repeat(count, body):
    if count == 1:
        body(0)
    elif count > 1:
        lax.fori_loop(0, count, lambda i, _: (body(i), 0)[1], 0)


def exchange_kernel(
    obj_hbm, probe_hbm, inten_hbm, pos, tabs_hbm,
    own_out, strip_out, left_out,
    obj_v, obj_b, probe_v, inten_v, tabs_v, strip_send, strip_recv, win, psi, lam, grad_send,
    obj_sem, load_sem, pos_sem, strip_ssem, strip_rsem, x_ssem, x_rsem, g_ssem, g_rsem,
    *, chunks, gchunks,
):
    cut, tile = lax.axis_index("cuts"), lax.axis_index("tile")
    ncut, ntile = lax.axis_size("cuts"), lax.axis_size("tile")
    per, _, rows, cols = obj_v.shape
    count, width = inten_v.shape[0], inten_v.shape[1]
    total = ncut * per
    height = width // chunks
    gheight = width // gchunks
    has_left, has_right = tile > 0, tile < ntile - 1
    left, right = {"tile": tile - 1}, {"tile": tile + 1}

    def obj_copy(j, part):
        return pltpu.make_async_copy(obj_hbm.at[j, part], obj_v.at[j, part], obj_sem.at[j, part])

    probe_copy = pltpu.make_async_copy(probe_hbm, probe_v, load_sem.at[1])
    tabs_copy = pltpu.make_async_copy(tabs_hbm, tabs_v, load_sem.at[2])
    inten_copy = pltpu.make_async_copy(inten_hbm, inten_v, load_sem.at[3])
    for j in range(per):
        for part in range(2):
            obj_copy(j, part).start()
    probe_copy.start()

    barrier = pltpu.get_barrier_semaphore()

    @pl.when(has_left)
    def _():
        pl.semaphore_signal(barrier, inc=1, device_id=left, device_id_type=MESH)

    @pl.when(has_right)
    def _():
        pl.semaphore_signal(barrier, inc=1, device_id=right, device_id_type=MESH)

    for o in range(1, ncut):
        peer = {"cuts": lax.rem(cut + o, ncut)}
        pl.semaphore_signal(barrier, inc=1, device_id=peer, device_id_type=MESH)
    peers = ncut - 1 + jnp.where(has_left, 1, 0) + jnp.where(has_right, 1, 0)
    pl.semaphore_wait(barrier, peers)

    pos_copy = pltpu.make_async_remote_copy(
        src_ref=pos, dst_ref=left_out, send_sem=pos_sem.at[0], recv_sem=pos_sem.at[1],
        device_id=right, device_id_type=MESH,
    )

    @pl.when(has_right)
    def _():
        pos_copy.start()

    lanes = lax.broadcasted_iota(jnp.int32, (height, cols), 1)
    glanes = lax.broadcasted_iota(jnp.int32, (gheight, cols), 1)
    unit = 128
    cell = lax.broadcasted_iota(jnp.int32, (width, unit), 1)
    line = lax.broadcasted_iota(jnp.int32, (width, unit), 0)

    def window_rows(row, first=0, size=width):
        base = row // LANE_ROWS * LANE_ROWS
        wanted = base + line + jnp.where(line < row - base, width, 0) - cell
        wanted = wanted[first : first + size]
        picks = [jnp.where(wanted == i * unit, 1.0, 0.0).astype(BF16) for i in range(rows // unit)]
        return dot(jnp.concatenate(picks, axis=1), obj_b[...]).astype(BF16)

    def strip_copy(p, k):
        span = pl.ds(k * height, height)
        return pltpu.make_async_remote_copy(
            src_ref=strip_send.at[p, :, :, span, :], dst_ref=strip_recv.at[p, :, :, span, :],
            send_sem=strip_ssem.at[p, k], recv_sem=strip_rsem.at[p, k],
            device_id=left, device_id_type=MESH,
        )

    def cross_copy(o, source, p, k):
        span = pl.ds(k * height, height)
        part = win.at[p, source, :, :, span, :]
        return pltpu.make_async_remote_copy(
            src_ref=part, dst_ref=part,
            send_sem=x_ssem.at[o - 1, p, k], recv_sem=x_rsem.at[o - 1, p, k],
            device_id={"cuts": lax.rem(cut + o, ncut)}, device_id_type=MESH,
        )

    def grad_copy(p, k):
        span = pl.ds(k * gheight, gheight)
        return pltpu.make_async_remote_copy(
            src_ref=grad_send.at[p, :, :, span, :], dst_ref=strip_out.at[p, :, :, span, :],
            send_sem=g_ssem.at[p, k], recv_sem=g_rsem.at[p, k],
            device_id=right, device_id_type=MESH,
        )

    for j in range(per):
        for part in range(2):
            obj_copy(j, part).wait()
            side = pl.ds((2 * j + part) * cols, cols)
            obj_b[:, side] = obj_v[j, part].astype(BF16)

    tabs_copy.start()
    inten_copy.start()

    @pl.when(has_left)
    def _():
        pos_copy.wait_recv()
        for p in range(count):
            steps = 2 if p == 0 else 1
            size = width // steps
            for step in range(steps):
                picked = window_rows(left_out[p, 0], step * size, size)
                for j in range(per):
                    for part in range(2):
                        first = (2 * j + part) * cols
                        strip_send[p, j, part, pl.ds(step * size, size), :] = picked[
                            :, first : first + cols
                        ]
                for k in range(step * chunks // steps, (step + 1) * chunks // steps):
                    strip_copy(p, k).start()

    @pl.when(jnp.logical_not(has_left))
    def _():
        for p in range(count):
            for d in range(2):
                left_out[p, d] = 0
        strip_out[...] = jnp.zeros_like(strip_out)

    @pl.when(jnp.logical_not(has_right))
    def _():
        strip_recv[...] = jnp.zeros_like(strip_recv)

    for p in range(count):
        picked = window_rows(pos[p, 0])
        for j in range(per):
            for part in range(2):
                first = (2 * j + part) * cols
                win[p, cut, j, part] = picked[:, first : first + cols]
        col = pos[p, 1] - tile * cols
        for k in range(chunks):

            @pl.when(has_right)
            def _():
                strip_copy(p, k).wait_recv()

            span = pl.ds(k * height, height)
            for j in range(per):
                for part in range(2):
                    win[p, cut, j, part, span, :] = jnp.where(
                        lanes >= col,
                        win[p, cut, j, part, span, :].astype(F32),
                        strip_recv[p, j, part, span, :].astype(F32),
                    ).astype(BF16)
            for o in range(1, ncut):
                cross_copy(o, cut, p, k).start()

    probe_copy.wait()
    across = lax.broadcasted_iota(jnp.int32, (width, width), 1)
    down = lax.broadcasted_iota(jnp.int32, (width, width), 0)
    for p in range(count):
        row, col = pos[p, 0], pos[p, 1] - tile * cols
        shift = row - row // LANE_ROWS * LANE_ROWS
        source = across + shift
        move_rows = jnp.where(jnp.where(source >= width, source - width, source) == down, 1.0, 0.0)
        source = down + col
        move_cols = jnp.where(jnp.where(source >= width, source - width, source) == across, 1.0, 0.0)
        for part in range(2):
            moved = dot(move_rows.astype(BF16), probe_v[part]).astype(BF16)
            psi[p, 0, part] = dot(moved, move_cols.astype(BF16)).astype(BF16)

    tabs_copy.wait()
    inten_copy.wait()

    def arrive(p, owner):
        @pl.when(owner != cut)
        def _():
            o = lax.rem(cut - owner + ncut, ncut)
            for k in range(chunks):
                cross_copy(o, owner, p, k).wait_recv()

    def sandwich(first, second, stacked):
        inner = dot(tabs_v[first], stacked).astype(BF16)
        side = jnp.concatenate([inner[:width], inner[width:]], axis=1)
        return dot(side, tabs_v[second])

    def exit_wave(p, s):
        owner, j = s // per, lax.rem(s, per)
        t_re = 1.0 + win[p, owner, j, 0].astype(F32)
        t_im = win[p, owner, j, 1].astype(F32)
        p_re, p_im = psi[p, s, 0].astype(F32), psi[p, s, 1].astype(F32)
        x_re = (p_re * t_re - p_im * t_im).astype(BF16)
        x_im = (p_re * t_im + p_im * t_re).astype(BF16)
        return jnp.concatenate([x_re, x_im], axis=0)

    def adjoint_slice(p, s, first, second, stacked):
        owner, j = s // per, lax.rem(s, per)
        col = pos[p, 1] - tile * cols
        inner = dot(tabs_v[first], stacked).astype(BF16)
        side = jnp.concatenate([inner[:width], inner[width:]], axis=1)

        @pl.when(owner == cut)
        def _():
            for k in range(gchunks):
                span = pl.ds(k * gheight, gheight)
                mu = dot(side[k * gheight : (k + 1) * gheight], tabs_v[second])
                m_re, m_im = mu[:, :width], mu[:, width:]
                p_re = psi[p, s, 0, span, :].astype(F32)
                p_im = psi[p, s, 1, span, :].astype(F32)
                g = (p_re * m_re + p_im * m_im, p_re * m_im - p_im * m_re)
                for part in range(2):
                    own_out[p, j, part, span, :] = jnp.where(glanes >= col, g[part], 0.0)
                    grad_send[p, j, part, span, :] = jnp.where(glanes >= col, 0.0, g[part]).astype(
                        BF16
                    )
                if per == 1:

                    @pl.when(has_right)
                    def _():
                        grad_copy(p, k).start()

        @pl.when(s > cut * per)
        def _():
            mu = dot(side, tabs_v[second])
            m_re, m_im = mu[:, :width], mu[:, width:]
            t_re = 1.0 + win[p, owner, j, 0].astype(F32)
            t_im = win[p, owner, j, 1].astype(F32)
            lam[:width] = (t_re * m_re + t_im * m_im).astype(BF16)
            lam[width:] = (t_re * m_im - t_im * m_re).astype(BF16)

    def one_probe(p):
        def forward(s):
            arrive(p, s // per)
            out = sandwich(0, 1, exit_wave(p, s))
            psi[p, s + 1, 0] = out[:, :width].astype(BF16)
            psi[p, s + 1, 1] = out[:, width:].astype(BF16)

        def backward(i):
            s = total - 2 - i

            @pl.when(s >= cut * per)
            def _():
                adjoint_slice(p, s, 1, 0, lam[...])

        if per == 1:
            repeat(total - 1, forward)
            arrive(p, total - 1)
        else:
            for s in range(ncut):
                arrive(p, s)
        adjoint_slice(p, total - 1, 3, 2, far_field(p))
        repeat(total - 1, backward)
        if per > 1:
            for k in range(gchunks):

                @pl.when(has_right)
                def _():
                    grad_copy(p, k).start()

    def far_field(p):
        out = sandwich(2, 3, exit_wave(p, total - 1))
        f_re, f_im = out[:, :width], out[:, width:]
        misfit = f_re * f_re + f_im * f_im - inten_v[p]
        return jnp.concatenate([(misfit * f_re).astype(BF16), (misfit * f_im).astype(BF16)], axis=0)

    for p in range(count):
        one_probe(p)

    @pl.when(has_right)
    def _():
        pos_copy.wait_send()
        for p in range(count):
            for k in range(gchunks):
                grad_copy(p, k).wait_send()

    for p in range(count):
        for k in range(chunks):
            for o in range(1, ncut):
                cross_copy(o, cut, p, k).wait_send()

    @pl.when(has_left)
    def _():
        for p in range(count):
            for k in range(chunks):
                strip_copy(p, k).wait_send()
        for p in range(count):
            for k in range(gchunks):
                grad_copy(p, k).wait_recv()


def place_kernel(own, strip, pos, left, out_hbm, out_v, sem):
    per, _, rows, cols = out_v.shape
    count, width = own.shape[0], own.shape[3]
    iota = lax.broadcasted_iota(jnp.int32, (LANE_ROWS, cols), 0)
    rest = width - LANE_ROWS

    def add(source, row, p, j, part):
        base = row // LANE_ROWS * LANE_ROWS
        shift = row - base
        body = pl.multiple_of(base + LANE_ROWS, LANE_ROWS)
        base = pl.multiple_of(base, LANE_ROWS)
        after = pl.multiple_of(jnp.minimum(base + width, rows - LANE_ROWS), LANE_ROWS)
        whole = source[p, j, part].astype(F32)
        out_v[j, part, pl.ds(body, rest), :] += whole[LANE_ROWS:]
        head = whole[:LANE_ROWS]
        out_v[j, part, pl.ds(base, LANE_ROWS), :] += jnp.where(iota >= shift, head, 0.0)
        out_v[j, part, pl.ds(after, LANE_ROWS), :] += jnp.where(iota < shift, head, 0.0)

    copies = []
    for j in range(per):
        for part in range(2):
            out_v[j, part] = jnp.zeros((rows, cols), F32)
            for p in range(count):
                add(own, pos[p, 0], p, j, part)
                add(strip, left[p, 0], p, j, part)
            copy = pltpu.make_async_copy(out_v.at[j, part], out_hbm.at[j, part], sem.at[j, part])
            copy.start()
            copies.append(copy)
    for copy in copies:
        copy.wait()


def per_device(tables, object_delta, probe_wave, intensity, positions):
    per, _, rows, cols = object_delta.shape
    count, width = intensity.shape[0], intensity.shape[1]
    ncut = lax.axis_size("cuts")
    chunks, gchunks = 8, 4
    anywhere = pl.BlockSpec(memory_space=pl.ANY)
    vmem = pl.BlockSpec(memory_space=pltpu.VMEM)
    smem = pl.BlockSpec(memory_space=pltpu.SMEM)
    dma = pltpu.SemaphoreType.DMA
    piece = (count, per, 2, width, cols)
    others = max(ncut - 1, 1)
    own, strip, left = pl.pallas_call(
        functools.partial(exchange_kernel, chunks=chunks, gchunks=gchunks),
        out_shape=(
            pltpu.VMEM(piece, F32),
            pltpu.VMEM(piece, BF16),
            jax.ShapeDtypeStruct(positions.shape, positions.dtype),
        ),
        in_specs=[anywhere, anywhere, anywhere, smem, anywhere],
        out_specs=(vmem, vmem, smem),
        scratch_shapes=[
            pltpu.VMEM(object_delta.shape, F32),
            pltpu.VMEM((rows, per * 2 * cols), BF16),
            pltpu.VMEM(probe_wave.shape, BF16),
            pltpu.VMEM(intensity.shape, F32),
            pltpu.VMEM(tables.shape, BF16),
            pltpu.VMEM(piece, BF16),
            pltpu.VMEM(piece, BF16),
            pltpu.VMEM((count, ncut, per, 2, width, cols), BF16),
            pltpu.VMEM((count, ncut * per, 2, width, cols), BF16),
            pltpu.VMEM((2 * width, cols), BF16),
            pltpu.VMEM(piece, BF16),
            dma((per, 2)),
            dma((4,)),
            dma((2,)),
            dma((count, chunks)),
            dma((count, chunks)),
            dma((others, count, chunks)),
            dma((others, count, chunks)),
            dma((count, gchunks)),
            dma((count, gchunks)),
        ],
        compiler_params=pltpu.CompilerParams(collective_id=0, has_side_effects=True),
        name="exchange",
    )(object_delta, probe_wave, intensity, positions, tables)
    own = pltpu.with_memory_space_constraint(own, pltpu.VMEM)
    strip = pltpu.with_memory_space_constraint(strip, pltpu.VMEM)
    return pl.pallas_call(
        place_kernel,
        out_shape=jax.ShapeDtypeStruct(object_delta.shape, F32),
        in_specs=[vmem, vmem, smem, smem],
        out_specs=anywhere,
        scratch_shapes=[pltpu.VMEM(object_delta.shape, F32), dma((per, 2))],
        name="place",
    )(own, strip, positions, left)


def solution(mesh):
    def whole(object_delta, probe_wave, intensity, positions):
        tables = jnp.asarray(make_tables(probe_wave.shape[-1]))
        return jax.shard_map(
            per_device,
            mesh=mesh,
            in_specs=(
                P(),
                P("cuts", None, None, "tile"),
                P(),
                P("tile", None, None),
                P("tile", None),
            ),
            out_specs=P("cuts", None, None, "tile"),
            check_vma=False,
        )(tables, object_delta, probe_wave, intensity, positions)

    return whole
```
